32 devices in a mesh: enc: 8 (over z, x), llm: 4 (over y, core).
Axes of the slice: x: 2, y: 2, z: 4, core: 2. Of those that a mesh axis runs over, the one named last changes fastest.
Arguments:
- patches: bfloat16 [4096, 5120], P('enc', 'llm'), may hold values from -6 to 6
- ln_gain: bfloat16 [1280], replicated, may hold values from 0.099609375 to 1.8984375
- w_in: bfloat16 [5120, 5120], P(None, 'llm'), may hold values from -0.078125 to 0.078125
- b_in: bfloat16 [5120], P('llm'), may hold values from -3 to 3
- w_out: bfloat16 [5120, 2048], P('llm'), may hold values from -0.078125 to 0.078125
- b_out: bfloat16 [2048], replicated, may hold values from -3 to 3
- owner: int32 [4096, 1], P(('enc', 'llm')), may hold values from 0 to 31; in each aligned block of 128 rows (0 to 127, 128 to 255, ...) at most 8 rows name the same one
- cotangent: bfloat16 [8192, 2048], P(('enc', 'llm')), may hold values from -6 to 6
Outputs:
- image_embeds: bfloat16 [8192, 2048], P(('enc', 'llm'))
- grad_w_in: float32 [5120, 5120], P('enc', 'llm')
- grad_w_out: float32 [5120, 2048], P('llm', 'enc')
- grad_patches: bfloat16 [4096, 5120], P('enc', 'llm')
The draws below stay inside these ranges and needn't reach their ends.
Inputs may be any that keep to these rules, and one draw needn't show every extreme that they name: Among the 128 consecutive tokens of one aligned block, no owner is named more than 8 times, a bound that some block reaches.
All inputs are finite; a program needn't handle non-finite values.
Results may differ from the reference program's by a relative error of at most 0.018.
Values may be sent and summed in bfloat16 or wider, within the bound.
A program may use at most 192 MiB of HBM per device.

```python
import math
import jax
import jax.numpy as jnp
import numpy as np
from jax import lax

VD = 1280
OD = 2048
MERGE = 4
TOK_ENC = 512
MH = 5120
TOKENS = 4096
CAP = 8
SLOTS = 256
N_ENC = 8
N_LLM = 4
DEVICES = 32


def spiked(entries, own_key, source, target, parts, factor):
    def block_of(axis_at):
        return (jnp.arange(entries.shape[axis_at]) // (entries.shape[axis_at] // parts)).reshape((-1,) + (1,) * (entries.ndim - 1 - axis_at))

    first = jax.random.permutation(own_key, parts)[block_of(target)]
    far = (block_of(target) + parts // 2) % parts
    return jnp.where((block_of(source) == first) | (block_of(source) == far), factor * entries, entries)


def block_levels(own_key, extent, split, low, high):
    loudness, own = 1.0, jax.random.fold_in(own_key, 6)
    for position, blocks in split:
        draws = jnp.exp(jax.random.uniform(jax.random.fold_in(own, position), (blocks,), jnp.float32, low / len(split), high / len(split)))
        loudness = loudness * jnp.repeat(draws, extent[position] // blocks).reshape([-1 if axis == position else 1 for axis in range(len(extent))])
    return loudness


def routed_block(key, own, number, rows, amount, top, bound, slope):
    ranking = jax.random.permutation(key, amount)
    heavy_load, ordinary = load_shares(amount, rows * top, bound, slope, True), load_shares(amount, rows * top, bound, slope, False)
    places = jnp.arange(amount)

    def named(lengths, offset_by):
        used = int((lengths > 0).sum())
        fixed = max(1, used // 4)
        shifted = fixed + (places - fixed + offset_by * (used - fixed)) % max(1, amount - fixed)
        return jnp.zeros((amount,), jnp.int32).at[ranking[jnp.where(places < fixed, places, shifted)]].set(jnp.asarray(lengths, jnp.int32))

    lengths = jnp.where(number % 4 == 0, named(heavy_load, number // 4), named(ordinary, number - number // 4 - 1))
    mixed = jax.random.permutation(jax.random.fold_in(own, 3), amount)
    giver, receiver = mixed[0:amount // 2 * 2:2], mixed[1:amount // 2 * 2:2]
    margin = jnp.minimum(lengths[giver] - 1, bound - lengths[receiver]) // 2
    margin = jnp.where((giver == ranking[0]) | (receiver == ranking[0]) | (lengths[receiver] == 0), 0, jnp.maximum(margin, 0))
    shifted = jax.random.randint(jax.random.fold_in(own, 4), (amount // 2,), 0, 1 << 20) % (margin + 1)
    lengths = lengths.at[giver].add(-shifted).at[receiver].add(shifted)
    members = jnp.searchsorted(jnp.cumsum(lengths), jnp.arange(rows * top), side="right").astype(jnp.int32)
    table = members.reshape(top, rows).T
    table = table[jax.random.permutation(jax.random.fold_in(own, 1), rows)]
    offset_by = jax.random.randint(jax.random.fold_in(own, 2), (rows, 1), 0, top)
    return jnp.take_along_axis(table, (jnp.arange(top)[None, :] + offset_by) % top, axis=1)


def load_shares(count, total, limit, slope, full):
    weights = [(1 << 20) // math.isqrt(rank ** slope) + 1 for rank in range(1, count + 1)]
    largest = limit if full else min(limit, max(-(-total // count), total * weights[0] // sum(weights)))
    least = 1 if total - largest >= count - 1 else 0
    counts, spare = [largest] + [least] * (count - 1), total - largest - least * (count - 1)
    while spare > 0:
        movable = [i for i in range(1, count) if counts[i] < largest] or [i for i in range(1, count) if counts[i] < limit]
        whole, remaining = sum([weights[i] for i in movable]), spare
        for i in movable:
            addition = min(limit - counts[i], max(1, remaining * weights[i] // whole), spare)
            counts[i] = counts[i] + addition
            spare = spare - addition
    return np.array(counts)


def centred(key, extent, spread, reach, split=(), kind=jnp.bfloat16):
    gain = block_levels(key, extent, split, -0.22, 0.18) if split else 1.0
    result = jax.random.normal(key, extent, jnp.float32) * spread * gain
    return jnp.minimum(jnp.maximum(result, -reach), reach).astype(kind)


def heavy_noise(rng, shape, width, most, cuts, heavy, kind=jnp.bfloat16):
    drawn = width * jax.random.normal(rng, shape, jnp.float32)
    if cuts:
        drawn = drawn * block_levels(rng, shape, cuts, -0.22, 0.18)
    return jnp.clip(spiked(drawn, jax.random.fold_in(rng, 3), *heavy), -most, most).astype(kind)


def setup_inputs(seed: int = 0) -> dict:
    splits = jax.random.split(jax.random.key(seed), 9)
    patches = heavy_noise(splits[0], (TOKENS, MH), 1.0, 6.0, ((0, 8), (1, 4)), (0, 1, 8, 2.0))
    ln_gain = jnp.clip(1.0 + 0.18 * jax.random.normal(splits[1], (VD,), jnp.float32), 0.099609375, 1.8984375).astype(jnp.bfloat16)
    w_in = centred(splits[2], (MH, MH), MH ** -0.5, 0.078125, ((1, 4),))
    b_in = centred(splits[3], (MH,), 0.5, 3.0, ((0, 4),))
    w_out = centred(splits[4], (MH, OD), MH ** -0.5, 0.078125, ((0, 4),))
    b_out = centred(splits[5], (OD,), 0.5, 3.0)
    owner_keys = jax.random.split(jax.random.fold_in(splits[6], 1), TOKENS // (TOKENS // DEVICES))
    owner_turns = jax.random.permutation(jax.random.fold_in(splits[6], 3), TOKENS // (TOKENS // DEVICES))
    owner = jax.vmap(lambda own, number: routed_block(jax.random.fold_in(splits[6], 2), own, number, TOKENS // DEVICES, DEVICES, 1, CAP, 2))(owner_keys, owner_turns).reshape((TOKENS, 1))
    cotangent = centred(splits[7], (DEVICES * SLOTS, OD), 1.0, 6.0, ((0, 32),))
    return {"patches": patches, "ln_gain": ln_gain, "w_in": w_in, "b_in": b_in, "w_out": w_out, "b_out": b_out, "owner": owner, "cotangent": cotangent}


EPSILON = 1e-06
HALF_ROOT = 0.7071067811865476
DENSITY = 0.3989422804014327

def gelu_slope(hidden):
    cdf = 0.5 * (1.0 + lax.erf(hidden * HALF_ROOT))
    return cdf + hidden * jnp.exp(-0.5 * hidden * hidden) * DENSITY

def reference(patches, ln_gain, w_in, b_in, w_out, b_out, owner, cotangent):
    devices = N_ENC * N_LLM
    own_rows = TOK_ENC // N_LLM
    merged = patches.astype(jnp.float32).reshape(TOKENS, MERGE, VD)
    inverse = lax.rsqrt(lax.optimization_barrier(jnp.mean(merged * merged, axis=-1, keepdims=True)) + EPSILON)
    normed = (merged * inverse * ln_gain.astype(jnp.float32)).reshape(TOKENS, MH).astype(jnp.bfloat16)
    hidden = jnp.dot(normed, w_in, preferred_element_type=jnp.float32) + b_in.astype(jnp.float32)
    active = jax.nn.gelu(hidden, approximate=False).astype(jnp.bfloat16)
    embeds = (jnp.dot(active, w_out, preferred_element_type=jnp.float32) + b_out.astype(jnp.float32)).astype(jnp.bfloat16)
    targets = owner[:, 0].astype(jnp.int32).reshape(devices, own_rows)
    before = jnp.arange(own_rows)[:, None] > jnp.arange(own_rows)[None, :]
    same_owner = targets[:, :, None] == targets[:, None, :]
    rank_in = lax.optimization_barrier(jnp.sum(jnp.logical_and(same_owner, before[None]), axis=2)).astype(jnp.int32)
    sources = jnp.arange(devices, dtype=jnp.int32)[:, None]
    slot_ids = (targets * (devices * CAP) + sources * CAP + rank_in).reshape(TOKENS).astype(jnp.int32)
    image_embeds = jnp.zeros((devices * devices * CAP, OD), jnp.bfloat16).at[slot_ids].set(embeds)
    grad_embeds = cotangent[slot_ids]
    grad_active = jnp.dot(grad_embeds, w_out.T, preferred_element_type=jnp.float32)
    grad_hidden = (grad_active * gelu_slope(hidden)).astype(jnp.bfloat16)

    def add_group(carry, items):
        normed_part, active_part, hidden_part, embeds_part = items
        in_part = jnp.dot(normed_part.T, hidden_part, preferred_element_type=jnp.float32).astype(jnp.bfloat16)
        out_part = jnp.dot(active_part.T, embeds_part, preferred_element_type=jnp.float32).astype(jnp.bfloat16)
        in_part, out_part = lax.optimization_barrier((in_part, out_part))
        return ((carry[0] + in_part.astype(jnp.float32), carry[1] + out_part.astype(jnp.float32)), None)
    zero_init = (jnp.zeros((MH, MH), jnp.float32), jnp.zeros((MH, OD), jnp.float32))
    items = (normed.reshape(N_ENC, TOK_ENC, MH), active.reshape(N_ENC, TOK_ENC, MH), grad_hidden.reshape(N_ENC, TOK_ENC, MH), grad_embeds.reshape(N_ENC, TOK_ENC, OD))
    (grad_w_in, grad_w_out), unused = lax.scan(add_group, zero_init, items)
    grad_normed = jnp.dot(grad_hidden, w_in.T, preferred_element_type=jnp.float32)
    scaled = grad_normed.reshape(TOKENS, MERGE, VD) * ln_gain.astype(jnp.float32)
    projection = lax.optimization_barrier(jnp.mean(scaled * merged, axis=-1, keepdims=True))
    cubed = inverse * inverse * inverse
    grad_patches = (inverse * scaled - merged * cubed * projection).reshape(TOKENS, MH).astype(jnp.bfloat16)
    return (image_embeds, grad_w_in, grad_w_out, grad_patches)
```

```python
import jax
import jax.numpy as jnp
from jax import lax
from jax.sharding import PartitionSpec as P

VD = 1280
MERGE = 4
SPLIT = 0.4


EPSILON = 1e-06
HALF_ROOT = 0.7071067811865476
DENSITY = 0.3989422804014327


def gelu_slope(hidden):
    cdf = 0.5 * (1.0 + lax.erf(hidden * HALF_ROOT))
    return cdf + hidden * jnp.exp(-0.5 * hidden * hidden) * DENSITY


def hop(value, axis, step, flip):
    pairs = lax.axis_size(axis) // 2
    table = [
        (2 * pair + member, 2 * ((pair + step) % pairs) + (member ^ flip))
        for pair in range(pairs)
        for member in range(2)
    ]
    return lax.ppermute(value, axis, table)


def wide_sum(*terms):
    total = terms[0].astype(jnp.float32)
    for term in terms[1:]:
        total = total + term.astype(jnp.float32)
    return total


def narrow_sum(*terms):
    return wide_sum(*terms).astype(jnp.bfloat16)


def ring_order(pairs):
    far = pairs // 2
    order = [far] + [k for near in range(far - 1, 0, -1) for k in (near, pairs - near)]
    return order + [0] if pairs > 1 else [0]


def ring_terms(part, axis, pairs):
    if pairs == 1:
        return [part[0]]
    if pairs == 2:
        return [part[0], hop(part[1], axis, 1, 0)]
    far = pairs // 2
    half = part[far].shape[0] // 2
    if pairs % 2:
        up, down = part[far], part[far + 1]
        start = far
    else:
        up, down = hop(part[far][:half], axis, 1, 0), hop(part[far][half:], axis, -1, 0)
        near, back = part[far - 1], part[(pairs - far + 1) % pairs]
        up = jnp.concatenate([narrow_sum(near[:half], up), near[half:]])
        down = jnp.concatenate([back[:half], narrow_sum(back[half:], down)])
        start = far - 1
    for k in range(start - 1, 0, -1):
        up = narrow_sum(part[k], hop(up, axis, 1, 0))
        down = narrow_sum(part[pairs - k], hop(down, axis, -1, 0))
    return [part[0], hop(up, axis, 1, 0), hop(down, axis, -1, 0)]


def pair_first(make, axis):
    pairs = lax.axis_size(axis) // 2
    part = {}
    for k in ring_order(pairs):
        arrived = hop(make(k, 1), axis, 0, 1)
        own = make(k, 0)
        part[k] = wide_sum(own, arrived) if k == 0 else narrow_sum(own, arrived)
    return wide_sum(*ring_terms(part, axis, pairs))


def ring_first(make_both, axis, rows):
    pairs = lax.axis_size(axis) // 2
    part = {k: make_both(k) for k in ring_order(pairs)}
    terms = ring_terms(part, axis, pairs)
    other = narrow_sum(*[term[:rows] for term in terms])
    return wide_sum(*[term[rows:] for term in terms], hop(other, axis, 0, 1))


def gather_chunks(own, axis):
    pairs = lax.axis_size(axis) // 2
    index = lax.axis_index(axis)
    pair, member = index // 2, index % 2
    chunks, current = [], own
    for k in range(pairs):
        source = (pair + pairs - k) % pairs
        chunks.append((2 * source + member, current))
        chunks.append((2 * source + 1 - member, hop(current, axis, 0, 1)))
        if k + 1 < pairs:
            current = hop(current, axis, 1, 0)
    return chunks


def assemble(chunks, dimension):
    size = chunks[0][1].shape[dimension]
    shape = list(chunks[0][1].shape)
    shape[dimension] = size * len(chunks)
    whole = jnp.zeros(shape, chunks[0][1].dtype)
    for index, chunk in chunks:
        whole = lax.dynamic_update_slice_in_dim(whole, chunk, index * size, dimension)
    return whole


def local(patches, ln_gain, w_in, b_in, w_out, b_out, owner, cotangent):
    group_size = lax.axis_size("llm")
    enc_size = lax.axis_size("enc")
    devices = enc_size * group_size
    slot_cap = cotangent.shape[0] // devices
    tokens = patches.shape[0]
    own_rows = tokens // group_size
    width = patches.shape[1]
    enc_pairs, llm_pairs = enc_size // 2, group_size // 2
    enc_index, llm_index = lax.axis_index("enc"), lax.axis_index("llm")

    def target(index, pairs, k, flip):
        return 2 * ((index // 2 + k) % pairs) + (index % 2 + flip) % 2

    own_count = width // VD
    gain = ln_gain.astype(jnp.float32)
    local_x = patches.astype(jnp.float32).reshape(tokens, own_count, VD)
    inverse = lax.rsqrt(jnp.mean(local_x * local_x, axis=-1, keepdims=True) + EPSILON)
    own_normed = (local_x * inverse * gain).reshape(tokens, width).astype(jnp.bfloat16)

    returned = lax.all_to_all(cotangent, ("enc", "llm"), split_axis=0, concat_axis=0, tiled=True)
    targets = owner[:, 0]
    before = jnp.arange(own_rows)[:, None] > jnp.arange(own_rows)[None, :]
    same_owner = targets[:, None] == targets[None, :]
    rank_in = jnp.sum(jnp.logical_and(same_owner, before), axis=1)
    slot_ids = targets * slot_cap + rank_in
    placing = (
        jnp.arange(devices * slot_cap, dtype=jnp.int32)[:, None] == slot_ids[None, :]
    ).astype(jnp.bfloat16)

    chunks = gather_chunks(own_normed, "llm")
    hidden = b_in.astype(jnp.float32)
    for index, chunk in chunks:
        rows = lax.dynamic_slice_in_dim(w_in, index * width, width, 0)
        hidden = hidden + jnp.dot(chunk, rows, preferred_element_type=jnp.float32)
    normed = assemble(chunks, 1)
    active = jax.nn.gelu(hidden, approximate=False).astype(jnp.bfloat16)
    slope = gelu_slope(hidden)

    own_grad = jnp.dot(placing.T, returned, preferred_element_type=jnp.float32).astype(jnp.bfloat16)
    grad_embeds = assemble(gather_chunks(own_grad, "llm"), 0)
    grad_active = lax.dot_general(
        grad_embeds, w_out, (((1,), (1,)), ((), ())), preferred_element_type=jnp.float32
    )
    grad_hidden = (grad_active * slope).astype(jnp.bfloat16)

    def product(left, right):
        return lax.dot_general(
            left, right, (((0,), (0,)), ((), ())), preferred_element_type=jnp.float32
        ).astype(jnp.bfloat16)

    out_cols = grad_embeds.shape[1] // enc_size
    cut = max(1, round(SPLIT * active.shape[1] / 128)) * 128
    active_a, active_b = active[:, :cut], active[:, cut:]

    def grad_cols(k, flip):
        return lax.dynamic_slice_in_dim(
            grad_embeds, target(enc_index, enc_pairs, k, flip) * out_cols, out_cols, 1
        )

    out_b = ring_first(
        lambda k: jnp.concatenate(
            [product(active_b, grad_cols(k, 1)), product(active_b, grad_cols(k, 0))]
        ),
        "enc",
        active_b.shape[1],
    )
    out_a = pair_first(lambda k, flip: product(active_a, grad_cols(k, flip)), "enc")
    grad_w_out = jnp.concatenate([out_a, out_b], axis=0)

    in_rows = normed.shape[1] // enc_size
    hidden_a, hidden_b = grad_hidden[:, :cut], grad_hidden[:, cut:]

    def normed_cols(k, flip):
        return lax.dynamic_slice_in_dim(
            normed, target(enc_index, enc_pairs, k, flip) * in_rows, in_rows, 1
        )

    in_b = ring_first(
        lambda k: product(
            jnp.concatenate([normed_cols(k, 1), normed_cols(k, 0)], axis=1), hidden_b
        ),
        "enc",
        in_rows,
    )
    in_a = pair_first(lambda k, flip: product(normed_cols(k, flip), hidden_a), "enc")
    grad_w_in = jnp.concatenate([in_a, in_b], axis=1)

    partial = jnp.dot(active, w_out, preferred_element_type=jnp.float32).astype(jnp.bfloat16)
    summed = pair_first(
        lambda k, flip: lax.dynamic_slice_in_dim(
            partial, target(llm_index, llm_pairs, k, flip) * own_rows, own_rows, 0
        ),
        "llm",
    )
    embeds = (summed + b_out.astype(jnp.float32)).astype(jnp.bfloat16)
    outgoing = jnp.dot(placing, embeds, preferred_element_type=jnp.float32).astype(jnp.bfloat16)
    image_embeds = lax.all_to_all(outgoing, ("enc", "llm"), split_axis=0, concat_axis=0, tiled=True)

    def feature(k, flip):
        rows = lax.dynamic_slice_in_dim(
            w_in, target(llm_index, llm_pairs, k, flip) * width, width, 0
        )
        return lax.dot_general(
            grad_hidden, rows, (((1,), (1,)), ((), ())), preferred_element_type=jnp.float32
        ).astype(jnp.bfloat16)

    grad_normed = pair_first(feature, "llm")
    scaled = grad_normed.reshape(tokens, own_count, VD) * gain
    projection = jnp.mean(scaled * local_x, axis=-1, keepdims=True)
    cubed = inverse * inverse * inverse
    grad_patches = (
        (inverse * scaled - local_x * cubed * projection)
        .reshape(tokens, own_count * VD)
        .astype(jnp.bfloat16)
    )
    return (image_embeds, grad_w_in, grad_w_out, grad_patches)


def solution(mesh):
    in_specs = (
        P("enc", "llm"),
        P(),
        P(None, "llm"),
        P("llm"),
        P("llm", None),
        P(),
        P(("enc", "llm"), None),
        P(("enc", "llm"), None),
    )
    out_specs = (P(("enc", "llm"), None), P("enc", "llm"), P("llm", "enc"), P("enc", "llm"))
    return jax.shard_map(local, mesh=mesh, in_specs=in_specs, out_specs=out_specs, check_vma=False)
```

```python
import jax
import jax.numpy as jnp
from jax import lax
from jax.sharding import PartitionSpec as P

VD = 1280
MERGE = 4
SPLIT = 0.8
CHAIN_MOST = 4


EPSILON = 1e-06
HALF_ROOT = 0.7071067811865476
DENSITY = 0.3989422804014327


def gelu_slope(hidden):
    cdf = 0.5 * (1.0 + lax.erf(hidden * HALF_ROOT))
    return cdf + hidden * jnp.exp(-0.5 * hidden * hidden) * DENSITY


def hop(value, axis, step, flip):
    pairs = lax.axis_size(axis) // 2
    table = [
        (2 * pair + member, 2 * ((pair + step) % pairs) + (member ^ flip))
        for pair in range(pairs)
        for member in range(2)
    ]
    return lax.ppermute(value, axis, table)


def line(value, axis, k, sign):
    pairs = lax.axis_size(axis) // 2
    table = [
        (2 * pair + member, 2 * (pair + sign) + member)
        for pair in range(pairs)
        if 0 <= pair + sign * k < pairs
        for member in range(2)
    ]
    return lax.ppermute(value, axis, table)


def wide_sum(*terms):
    total = terms[0].astype(jnp.float32)
    for term in terms[1:]:
        total = total + term.astype(jnp.float32)
    return total


def narrow_sum(*terms):
    return wide_sum(*terms).astype(jnp.bfloat16)


def ring_order(pairs):
    if 2 < pairs <= CHAIN_MOST:
        return [k for far in range(pairs - 1, pairs // 2, -1) for k in (far, pairs - far)] + (
            [pairs // 2] if pairs % 2 == 0 else []
        ) + [0]
    far = pairs // 2
    order = [far] + [k for near in range(far - 1, 0, -1) for k in (near, pairs - near)]
    return order + [0] if pairs > 1 else [0]


def ring_terms(part, axis, pairs):
    if pairs == 1:
        return [part[0]]
    if pairs == 2:
        return [part[0], hop(part[1], axis, 1, 0)]
    if pairs <= CHAIN_MOST:
        up, down = line(part[pairs - 1], axis, pairs - 1, 1), line(part[1], axis, pairs - 1, -1)
        for k in range(pairs - 2, 0, -1):
            up = line(narrow_sum(part[k], up), axis, k, 1)
            down = line(narrow_sum(part[pairs - k], down), axis, k, -1)
        return [part[0], up, down]
    far = pairs // 2
    half = part[far].shape[0] // 2
    if pairs % 2:
        up, down = part[far], part[far + 1]
        start = far
    else:
        up, down = hop(part[far][:half], axis, 1, 0), hop(part[far][half:], axis, -1, 0)
        near, back = part[far - 1], part[(pairs - far + 1) % pairs]
        up = jnp.concatenate([narrow_sum(near[:half], up), near[half:]])
        down = jnp.concatenate([back[:half], narrow_sum(back[half:], down)])
        start = far - 1
    for k in range(start - 1, 0, -1):
        up = narrow_sum(part[k], hop(up, axis, 1, 0))
        down = narrow_sum(part[pairs - k], hop(down, axis, -1, 0))
    return [part[0], hop(up, axis, 1, 0), hop(down, axis, -1, 0)]


def pair_first(make, axis):
    pairs = lax.axis_size(axis) // 2
    part = {}
    for k in ring_order(pairs):
        arrived = hop(make(k, 1), axis, 0, 1)
        own = make(k, 0)
        part[k] = wide_sum(own, arrived) if k == 0 else narrow_sum(own, arrived)
    return wide_sum(*ring_terms(part, axis, pairs))


def ring_first(make_both, axis, rows):
    pairs = lax.axis_size(axis) // 2
    part = {k: make_both(k) for k in ring_order(pairs)}
    terms = ring_terms(part, axis, pairs)
    other = narrow_sum(*[term[:rows] for term in terms])
    return wide_sum(*[term[rows:] for term in terms], hop(other, axis, 0, 1))


def gather_chunks(own, axis):
    pairs = lax.axis_size(axis) // 2
    index = lax.axis_index(axis)
    pair, member = index // 2, index % 2
    chunks, current = [], own
    for k in range(pairs):
        source = (pair + pairs - k) % pairs
        chunks.append((2 * source + member, current))
        chunks.append((2 * source + 1 - member, hop(current, axis, 0, 1)))
        if k + 1 < pairs:
            current = hop(current, axis, 1, 0)
    return chunks


def assemble(chunks, dimension):
    size = chunks[0][1].shape[dimension]
    shape = list(chunks[0][1].shape)
    shape[dimension] = size * len(chunks)
    whole = jnp.zeros(shape, chunks[0][1].dtype)
    for index, chunk in chunks:
        whole = lax.dynamic_update_slice_in_dim(whole, chunk, index * size, dimension)
    return whole


def local(patches, ln_gain, w_in, b_in, w_out, b_out, owner, cotangent):
    group_size = lax.axis_size("llm")
    enc_size = lax.axis_size("enc")
    devices = enc_size * group_size
    slot_cap = cotangent.shape[0] // devices
    tokens = patches.shape[0]
    own_rows = tokens // group_size
    width = patches.shape[1]
    enc_pairs, llm_pairs = enc_size // 2, group_size // 2
    enc_index, llm_index = lax.axis_index("enc"), lax.axis_index("llm")

    def target(index, pairs, k, flip):
        return 2 * ((index // 2 + k) % pairs) + (index % 2 + flip) % 2

    own_count = width // VD
    gain = ln_gain.astype(jnp.float32)
    local_x = patches.astype(jnp.float32).reshape(tokens, own_count, VD)
    inverse = lax.rsqrt(jnp.mean(local_x * local_x, axis=-1, keepdims=True) + EPSILON)
    own_normed = (local_x * inverse * gain).reshape(tokens, width).astype(jnp.bfloat16)

    returned = lax.all_to_all(cotangent, ("enc", "llm"), split_axis=0, concat_axis=0, tiled=True)
    targets = owner[:, 0]
    before = jnp.arange(own_rows)[:, None] > jnp.arange(own_rows)[None, :]
    same_owner = targets[:, None] == targets[None, :]
    rank_in = jnp.sum(jnp.logical_and(same_owner, before), axis=1)
    slot_ids = targets * slot_cap + rank_in
    placing = (
        jnp.arange(devices * slot_cap, dtype=jnp.int32)[:, None] == slot_ids[None, :]
    ).astype(jnp.bfloat16)

    chunks = gather_chunks(own_normed, "llm")
    hidden = b_in.astype(jnp.float32)
    for index, chunk in chunks:
        rows = lax.dynamic_slice_in_dim(w_in, index * width, width, 0)
        hidden = hidden + jnp.dot(chunk, rows, preferred_element_type=jnp.float32)
    normed = assemble(chunks, 1)
    active = jax.nn.gelu(hidden, approximate=False).astype(jnp.bfloat16)
    slope = gelu_slope(hidden)

    own_grad = jnp.dot(placing.T, returned, preferred_element_type=jnp.float32).astype(jnp.bfloat16)
    grad_embeds = assemble(gather_chunks(own_grad, "llm"), 0)
    grad_active = lax.dot_general(
        grad_embeds, w_out, (((1,), (1,)), ((), ())), preferred_element_type=jnp.float32
    )
    grad_hidden = (grad_active * slope).astype(jnp.bfloat16)

    def product(left, right):
        return lax.dot_general(
            left, right, (((0,), (0,)), ((), ())), preferred_element_type=jnp.float32
        ).astype(jnp.bfloat16)

    out_cols = grad_embeds.shape[1] // enc_size
    grad_w_out = pair_first(
        lambda k, flip: product(
            active,
            lax.dynamic_slice_in_dim(
                grad_embeds, target(enc_index, enc_pairs, k, flip) * out_cols, out_cols, 1
            ),
        ),
        "enc",
    )

    in_rows = normed.shape[1] // enc_size
    cut = max(1, round(SPLIT * grad_hidden.shape[1] / 128)) * 128
    hidden_a, hidden_b = grad_hidden[:, :cut], grad_hidden[:, cut:]

    def normed_cols(k, flip):
        return lax.dynamic_slice_in_dim(
            normed, target(enc_index, enc_pairs, k, flip) * in_rows, in_rows, 1
        )

    in_b = ring_first(
        lambda k: product(
            jnp.concatenate([normed_cols(k, 1), normed_cols(k, 0)], axis=1), hidden_b
        ),
        "enc",
        in_rows,
    )
    in_a = pair_first(lambda k, flip: product(normed_cols(k, flip), hidden_a), "enc")
    grad_w_in = jnp.concatenate([in_a, in_b], axis=1)

    partial = jnp.dot(active, w_out, preferred_element_type=jnp.float32).astype(jnp.bfloat16)
    summed = pair_first(
        lambda k, flip: lax.dynamic_slice_in_dim(
            partial, target(llm_index, llm_pairs, k, flip) * own_rows, own_rows, 0
        ),
        "llm",
    )
    embeds = (summed + b_out.astype(jnp.float32)).astype(jnp.bfloat16)
    outgoing = jnp.dot(placing, embeds, preferred_element_type=jnp.float32).astype(jnp.bfloat16)
    image_embeds = lax.all_to_all(outgoing, ("enc", "llm"), split_axis=0, concat_axis=0, tiled=True)

    def feature(k, flip):
        rows = lax.dynamic_slice_in_dim(
            w_in, target(llm_index, llm_pairs, k, flip) * width, width, 0
        )
        return lax.dot_general(
            grad_hidden, rows, (((1,), (1,)), ((), ())), preferred_element_type=jnp.float32
        ).astype(jnp.bfloat16)

    grad_normed = pair_first(feature, "llm")
    scaled = grad_normed.reshape(tokens, own_count, VD) * gain
    projection = jnp.mean(scaled * local_x, axis=-1, keepdims=True)
    cubed = inverse * inverse * inverse
    grad_patches = (
        (inverse * scaled - local_x * cubed * projection)
        .reshape(tokens, own_count * VD)
        .astype(jnp.bfloat16)
    )
    return (image_embeds, grad_w_in, grad_w_out, grad_patches)


def solution(mesh):
    in_specs = (
        P("enc", "llm"),
        P(),
        P(None, "llm"),
        P("llm"),
        P("llm", None),
        P(),
        P(("enc", "llm"), None),
        P(("enc", "llm"), None),
    )
    out_specs = (P(("enc", "llm"), None), P("enc", "llm"), P("llm", "enc"), P("enc", "llm"))
    return jax.shard_map(local, mesh=mesh, in_specs=in_specs, out_specs=out_specs, check_vma=False)
```

```python
import jax
import jax.numpy as jnp
from jax import lax
from jax.sharding import PartitionSpec as P

VD = 1280
MERGE = 4
SPLIT = 0.8
CHAIN_MOST = 4


EPSILON = 1e-06
HALF_ROOT = 0.7071067811865476
DENSITY = 0.3989422804014327


def gelu_slope(hidden):
    cdf = 0.5 * (1.0 + lax.erf(hidden * HALF_ROOT))
    return cdf + hidden * jnp.exp(-0.5 * hidden * hidden) * DENSITY


def hop(value, axis, step, flip):
    pairs = lax.axis_size(axis) // 2
    table = [
        (2 * pair + member, 2 * ((pair + step) % pairs) + (member ^ flip))
        for pair in range(pairs)
        for member in range(2)
    ]
    return lax.ppermute(value, axis, table)


def line(value, axis, k, sign):
    pairs = lax.axis_size(axis) // 2
    table = [
        (2 * pair + member, 2 * (pair + sign) + member)
        for pair in range(pairs)
        if 0 <= pair + sign * k < pairs
        for member in range(2)
    ]
    return lax.ppermute(value, axis, table)


def wide_sum(*terms):
    total = terms[0].astype(jnp.float32)
    for term in terms[1:]:
        total = total + term.astype(jnp.float32)
    return total


def narrow_sum(*terms):
    return wide_sum(*terms).astype(jnp.bfloat16)


def ring_order(pairs):
    if 2 < pairs <= CHAIN_MOST:
        return [k for far in range(pairs - 1, pairs // 2, -1) for k in (far, pairs - far)] + (
            [pairs // 2] if pairs % 2 == 0 else []
        ) + [0]
    far = pairs // 2
    order = [far] + [k for near in range(far - 1, 0, -1) for k in (near, pairs - near)]
    return order + [0] if pairs > 1 else [0]


def ring_terms(part, axis, pairs):
    if pairs == 1:
        return [part[0]]
    if pairs == 2:
        return [part[0], hop(part[1], axis, 1, 0)]
    if pairs <= CHAIN_MOST:
        up, down = line(part[pairs - 1], axis, pairs - 1, 1), line(part[1], axis, pairs - 1, -1)
        for k in range(pairs - 2, 0, -1):
            up = line(narrow_sum(part[k], up), axis, k, 1)
            down = line(narrow_sum(part[pairs - k], down), axis, k, -1)
        return [part[0], up, down]
    far = pairs // 2
    half = part[far].shape[0] // 2
    if pairs % 2:
        up, down = part[far], part[far + 1]
        start = far
    else:
        up, down = hop(part[far][:half], axis, 1, 0), hop(part[far][half:], axis, -1, 0)
        near, back = part[far - 1], part[(pairs - far + 1) % pairs]
        up = jnp.concatenate([narrow_sum(near[:half], up), near[half:]])
        down = jnp.concatenate([back[:half], narrow_sum(back[half:], down)])
        start = far - 1
    for k in range(start - 1, 0, -1):
        up = narrow_sum(part[k], hop(up, axis, 1, 0))
        down = narrow_sum(part[pairs - k], hop(down, axis, -1, 0))
    return [part[0], hop(up, axis, 1, 0), hop(down, axis, -1, 0)]


def pair_firsts(makes, axis):
    pairs = lax.axis_size(axis) // 2
    order = [(number, k) for number in range(len(makes)) for k in ring_order(pairs)]
    arrived = []
    for place, (number, k) in enumerate(order):
        value = makes[number](k, 1)
        if place >= 2:
            value, arrived[place - 2] = lax.optimization_barrier((value, arrived[place - 2]))
        arrived.append(hop(value, axis, 0, 1))
    parts = [{} for make in makes]
    for (number, k), received in zip(order, arrived):
        own = makes[number](k, 0)
        parts[number][k] = wide_sum(own, received) if k == 0 else narrow_sum(own, received)
    return [wide_sum(*ring_terms(part, axis, pairs)) for part in parts]


def ring_first(make_both, axis, rows):
    pairs = lax.axis_size(axis) // 2
    part = {k: make_both(k) for k in ring_order(pairs)}
    terms = ring_terms(part, axis, pairs)
    other = narrow_sum(*[term[:rows] for term in terms])
    return wide_sum(*[term[rows:] for term in terms], hop(other, axis, 0, 1))


def gather_chunks(own, axis):
    pairs = lax.axis_size(axis) // 2
    index = lax.axis_index(axis)
    pair, member = index // 2, index % 2
    chunks, current = [], own
    for k in range(pairs):
        source = (pair + pairs - k) % pairs
        chunks.append((2 * source + member, current))
        chunks.append((2 * source + 1 - member, hop(current, axis, 0, 1)))
        if k + 1 < pairs:
            current = hop(current, axis, 1, 0)
    return chunks


def assemble(chunks, dimension):
    size = chunks[0][1].shape[dimension]
    shape = list(chunks[0][1].shape)
    shape[dimension] = size * len(chunks)
    whole = jnp.zeros(shape, chunks[0][1].dtype)
    for index, chunk in chunks:
        whole = lax.dynamic_update_slice_in_dim(whole, chunk, index * size, dimension)
    return whole


def local(patches, ln_gain, w_in, b_in, w_out, b_out, owner, cotangent):
    group_size = lax.axis_size("llm")
    enc_size = lax.axis_size("enc")
    devices = enc_size * group_size
    slot_cap = cotangent.shape[0] // devices
    tokens = patches.shape[0]
    own_rows = tokens // group_size
    width = patches.shape[1]
    enc_pairs, llm_pairs = enc_size // 2, group_size // 2
    enc_index, llm_index = lax.axis_index("enc"), lax.axis_index("llm")

    def target(index, pairs, k, flip):
        return 2 * ((index // 2 + k) % pairs) + (index % 2 + flip) % 2

    own_count = width // VD
    gain = ln_gain.astype(jnp.float32)
    local_x = patches.astype(jnp.float32).reshape(tokens, own_count, VD)
    inverse = lax.rsqrt(jnp.mean(local_x * local_x, axis=-1, keepdims=True) + EPSILON)
    own_normed = (local_x * inverse * gain).reshape(tokens, width).astype(jnp.bfloat16)

    returned = lax.all_to_all(cotangent, ("enc", "llm"), split_axis=0, concat_axis=0, tiled=True)
    targets = owner[:, 0]
    before = jnp.arange(own_rows)[:, None] > jnp.arange(own_rows)[None, :]
    same_owner = targets[:, None] == targets[None, :]
    rank_in = jnp.sum(jnp.logical_and(same_owner, before), axis=1)
    slot_ids = targets * slot_cap + rank_in
    placing = (
        jnp.arange(devices * slot_cap, dtype=jnp.int32)[:, None] == slot_ids[None, :]
    ).astype(jnp.bfloat16)

    chunks = gather_chunks(own_normed, "llm")
    hidden = b_in.astype(jnp.float32)
    for index, chunk in chunks:
        rows = lax.dynamic_slice_in_dim(w_in, index * width, width, 0)
        hidden = hidden + jnp.dot(chunk, rows, preferred_element_type=jnp.float32)
    normed = assemble(chunks, 1)
    active = jax.nn.gelu(hidden, approximate=False).astype(jnp.bfloat16)
    slope = gelu_slope(hidden)

    own_grad = jnp.dot(placing.T, returned, preferred_element_type=jnp.float32).astype(jnp.bfloat16)
    grad_embeds = assemble(gather_chunks(own_grad, "llm"), 0)
    grad_active = lax.dot_general(
        grad_embeds, w_out, (((1,), (1,)), ((), ())), preferred_element_type=jnp.float32
    )
    grad_hidden = (grad_active * slope).astype(jnp.bfloat16)

    def product(left, right):
        return lax.dot_general(
            left, right, (((0,), (0,)), ((), ())), preferred_element_type=jnp.float32
        ).astype(jnp.bfloat16)

    out_cols = grad_embeds.shape[1] // enc_size

    def out_term(k, flip):
        columns = lax.dynamic_slice_in_dim(
            grad_embeds, target(enc_index, enc_pairs, k, flip) * out_cols, out_cols, 1
        )
        return product(active, columns)

    in_rows = normed.shape[1] // enc_size
    cut = max(1, round(SPLIT * grad_hidden.shape[1] / 128)) * 128
    hidden_a, hidden_b = grad_hidden[:, :cut], grad_hidden[:, cut:]

    def normed_cols(k, flip):
        return lax.dynamic_slice_in_dim(
            normed, target(enc_index, enc_pairs, k, flip) * in_rows, in_rows, 1
        )

    in_b = ring_first(
        lambda k: product(
            jnp.concatenate([normed_cols(k, 1), normed_cols(k, 0)], axis=1), hidden_b
        ),
        "enc",
        in_rows,
    )
    grad_w_out, in_a = pair_firsts(
        [out_term, lambda k, flip: product(normed_cols(k, flip), hidden_a)], "enc"
    )
    grad_w_in = jnp.concatenate([in_a, in_b], axis=1)

    partial = jnp.dot(active, w_out, preferred_element_type=jnp.float32).astype(jnp.bfloat16)
    summed = pair_firsts(
        [lambda k, flip: lax.dynamic_slice_in_dim(
            partial, target(llm_index, llm_pairs, k, flip) * own_rows, own_rows, 0
        )],
        "llm",
    )[0]
    embeds = (summed + b_out.astype(jnp.float32)).astype(jnp.bfloat16)
    outgoing = jnp.dot(placing, embeds, preferred_element_type=jnp.float32).astype(jnp.bfloat16)
    image_embeds = lax.all_to_all(outgoing, ("enc", "llm"), split_axis=0, concat_axis=0, tiled=True)

    def feature(k, flip):
        rows = lax.dynamic_slice_in_dim(
            w_in, target(llm_index, llm_pairs, k, flip) * width, width, 0
        )
        return lax.dot_general(
            grad_hidden, rows, (((1,), (1,)), ((), ())), preferred_element_type=jnp.float32
        ).astype(jnp.bfloat16)

    grad_normed = pair_firsts([feature], "llm")[0]
    scaled = grad_normed.reshape(tokens, own_count, VD) * gain
    projection = jnp.mean(scaled * local_x, axis=-1, keepdims=True)
    cubed = inverse * inverse * inverse
    grad_patches = (
        (inverse * scaled - local_x * cubed * projection)
        .reshape(tokens, own_count * VD)
        .astype(jnp.bfloat16)
    )
    return (image_embeds, grad_w_in, grad_w_out, grad_patches)


def solution(mesh):
    in_specs = (
        P("enc", "llm"),
        P(),
        P(None, "llm"),
        P("llm"),
        P("llm", None),
        P(),
        P(("enc", "llm"), None),
        P(("enc", "llm"), None),
    )
    out_specs = (P(("enc", "llm"), None), P("enc", "llm"), P("llm", "enc"), P("enc", "llm"))
    return jax.shard_map(local, mesh=mesh, in_specs=in_specs, out_specs=out_specs, check_vma=False)
```

```python
import jax
import jax.numpy as jnp
from jax import lax
from jax.sharding import PartitionSpec as P

VD = 1280
MERGE = 4
SPLIT = 0.7
CHAIN_MOST = 4


EPSILON = 1e-06
HALF_ROOT = 0.7071067811865476
DENSITY = 0.3989422804014327


def gelu_slope(hidden):
    cdf = 0.5 * (1.0 + lax.erf(hidden * HALF_ROOT))
    return cdf + hidden * jnp.exp(-0.5 * hidden * hidden) * DENSITY


def hop(value, axis, step, flip):
    pairs = lax.axis_size(axis) // 2
    table = [
        (2 * pair + member, 2 * ((pair + step) % pairs) + (member ^ flip))
        for pair in range(pairs)
        for member in range(2)
    ]
    return lax.ppermute(value, axis, table)


def line(value, axis, k, sign):
    pairs = lax.axis_size(axis) // 2
    table = [
        (2 * pair + member, 2 * (pair + sign) + member)
        for pair in range(pairs)
        if 0 <= pair + sign * k < pairs
        for member in range(2)
    ]
    return lax.ppermute(value, axis, table)


def wide_sum(*terms):
    total = terms[0].astype(jnp.float32)
    for term in terms[1:]:
        total = total + term.astype(jnp.float32)
    return total


def narrow_sum(*terms):
    return wide_sum(*terms).astype(jnp.bfloat16)


def ring_order(pairs):
    if 2 < pairs <= CHAIN_MOST:
        return [k for far in range(pairs - 1, pairs // 2, -1) for k in (far, pairs - far)] + (
            [pairs // 2] if pairs % 2 == 0 else []
        ) + [0]
    far = pairs // 2
    order = [far] + [k for near in range(far - 1, 0, -1) for k in (near, pairs - near)]
    return order + [0] if pairs > 1 else [0]


def ring_terms(part, axis, pairs):
    if pairs == 1:
        return [part[0]]
    if pairs == 2:
        return [part[0], hop(part[1], axis, 1, 0)]
    if pairs <= CHAIN_MOST:
        up, down = line(part[pairs - 1], axis, pairs - 1, 1), line(part[1], axis, pairs - 1, -1)
        for k in range(pairs - 2, 0, -1):
            up = line(narrow_sum(part[k], up), axis, k, 1)
            down = line(narrow_sum(part[pairs - k], down), axis, k, -1)
        return [part[0], up, down]
    far = pairs // 2
    half = part[far].shape[0] // 2
    if pairs % 2:
        up, down = part[far], part[far + 1]
        start = far
    else:
        up, down = hop(part[far][:half], axis, 1, 0), hop(part[far][half:], axis, -1, 0)
        near, back = part[far - 1], part[(pairs - far + 1) % pairs]
        up = jnp.concatenate([narrow_sum(near[:half], up), near[half:]])
        down = jnp.concatenate([back[:half], narrow_sum(back[half:], down)])
        start = far - 1
    for k in range(start - 1, 0, -1):
        up = narrow_sum(part[k], hop(up, axis, 1, 0))
        down = narrow_sum(part[pairs - k], hop(down, axis, -1, 0))
    return [part[0], hop(up, axis, 1, 0), hop(down, axis, -1, 0)]


def pair_firsts(makes, axis):
    pairs = lax.axis_size(axis) // 2
    order = [(number, k) for number in range(len(makes)) for k in ring_order(pairs)]
    arrived = []
    for place, (number, k) in enumerate(order):
        value = makes[number](k, 1)
        if place >= 2:
            value, arrived[place - 2] = lax.optimization_barrier((value, arrived[place - 2]))
        arrived.append(hop(value, axis, 0, 1))
    parts = [{} for make in makes]
    for (number, k), received in zip(order, arrived):
        own = makes[number](k, 0)
        parts[number][k] = wide_sum(own, received) if k == 0 else narrow_sum(own, received)
    return [wide_sum(*ring_terms(part, axis, pairs)) for part in parts]


def ring_first(make_both, axis, rows):
    pairs = lax.axis_size(axis) // 2
    part = {k: make_both(k) for k in ring_order(pairs)}
    terms = ring_terms(part, axis, pairs)
    other = narrow_sum(*[term[:rows] for term in terms])
    return wide_sum(*[term[rows:] for term in terms], hop(other, axis, 0, 1))


def gather_chunks(own, axis):
    pairs = lax.axis_size(axis) // 2
    index = lax.axis_index(axis)
    pair, member = index // 2, index % 2
    chunks, current = [], own
    for k in range(pairs):
        source = (pair + pairs - k) % pairs
        chunks.append((2 * source + member, current))
        chunks.append((2 * source + 1 - member, hop(current, axis, 0, 1)))
        if k + 1 < pairs:
            current = hop(current, axis, 1, 0)
    return chunks


def assemble(chunks, dimension):
    size = chunks[0][1].shape[dimension]
    shape = list(chunks[0][1].shape)
    shape[dimension] = size * len(chunks)
    whole = jnp.zeros(shape, chunks[0][1].dtype)
    for index, chunk in chunks:
        whole = lax.dynamic_update_slice_in_dim(whole, chunk, index * size, dimension)
    return whole


def local(patches, ln_gain, w_in, b_in, w_out, b_out, owner, cotangent):
    group_size = lax.axis_size("llm")
    enc_size = lax.axis_size("enc")
    devices = enc_size * group_size
    slot_cap = cotangent.shape[0] // devices
    tokens = patches.shape[0]
    own_rows = tokens // group_size
    width = patches.shape[1]
    enc_pairs, llm_pairs = enc_size // 2, group_size // 2
    enc_index, llm_index = lax.axis_index("enc"), lax.axis_index("llm")

    def target(index, pairs, k, flip):
        return 2 * ((index // 2 + k) % pairs) + (index % 2 + flip) % 2

    own_count = width // VD
    gain = ln_gain.astype(jnp.float32)
    local_x = patches.astype(jnp.float32).reshape(tokens, own_count, VD)
    inverse = lax.rsqrt(jnp.mean(local_x * local_x, axis=-1, keepdims=True) + EPSILON)
    own_normed = (local_x * inverse * gain).reshape(tokens, width).astype(jnp.bfloat16)

    returned = lax.all_to_all(cotangent, ("enc", "llm"), split_axis=0, concat_axis=0, tiled=True)
    targets = owner[:, 0]
    before = jnp.arange(own_rows)[:, None] > jnp.arange(own_rows)[None, :]
    same_owner = targets[:, None] == targets[None, :]
    rank_in = jnp.sum(jnp.logical_and(same_owner, before), axis=1)
    slot_ids = targets * slot_cap + rank_in
    placing = (
        jnp.arange(devices * slot_cap, dtype=jnp.int32)[:, None] == slot_ids[None, :]
    ).astype(jnp.bfloat16)

    chunks = gather_chunks(own_normed, "llm")
    hidden = b_in.astype(jnp.float32)
    for index, chunk in chunks:
        rows = lax.dynamic_slice_in_dim(w_in, index * width, width, 0)
        hidden = hidden + jnp.dot(chunk, rows, preferred_element_type=jnp.float32)
    normed = assemble(chunks, 1)
    active = jax.nn.gelu(hidden, approximate=False).astype(jnp.bfloat16)
    slope = gelu_slope(hidden)

    own_grad = jnp.dot(placing.T, returned, preferred_element_type=jnp.float32).astype(jnp.bfloat16)
    grad_embeds = assemble(gather_chunks(own_grad, "llm"), 0)
    grad_active = lax.dot_general(
        grad_embeds, w_out, (((1,), (1,)), ((), ())), preferred_element_type=jnp.float32
    )
    grad_hidden = (grad_active * slope).astype(jnp.bfloat16)

    def product(left, right):
        return lax.dot_general(
            left, right, (((0,), (0,)), ((), ())), preferred_element_type=jnp.float32
        ).astype(jnp.bfloat16)

    out_cols = grad_embeds.shape[1] // enc_size

    def out_term(k, flip):
        columns = lax.dynamic_slice_in_dim(
            grad_embeds, target(enc_index, enc_pairs, k, flip) * out_cols, out_cols, 1
        )
        return product(active, columns)

    in_rows = normed.shape[1] // enc_size
    cut = max(1, round(SPLIT * grad_hidden.shape[1] / 128)) * 128
    hidden_a, hidden_b = grad_hidden[:, :cut], grad_hidden[:, cut:]

    def normed_cols(k, flip):
        return lax.dynamic_slice_in_dim(
            normed, target(enc_index, enc_pairs, k, flip) * in_rows, in_rows, 1
        )

    in_b = ring_first(
        lambda k: product(
            jnp.concatenate([normed_cols(k, 1), normed_cols(k, 0)], axis=1), hidden_b
        ),
        "enc",
        in_rows,
    )
    grad_w_out, in_a = pair_firsts(
        [out_term, lambda k, flip: product(normed_cols(k, flip), hidden_a)], "enc"
    )
    grad_w_in = jnp.concatenate([in_a, in_b], axis=1)

    partial = jnp.dot(active, w_out, preferred_element_type=jnp.float32).astype(jnp.bfloat16)
    summed = pair_firsts(
        [lambda k, flip: lax.dynamic_slice_in_dim(
            partial, target(llm_index, llm_pairs, k, flip) * own_rows, own_rows, 0
        )],
        "llm",
    )[0]
    embeds = (summed + b_out.astype(jnp.float32)).astype(jnp.bfloat16)
    outgoing = jnp.dot(placing, embeds, preferred_element_type=jnp.float32).astype(jnp.bfloat16)
    image_embeds = lax.all_to_all(outgoing, ("enc", "llm"), split_axis=0, concat_axis=0, tiled=True)

    def feature(k, flip):
        rows = lax.dynamic_slice_in_dim(
            w_in, target(llm_index, llm_pairs, k, flip) * width, width, 0
        )
        return lax.dot_general(
            grad_hidden, rows, (((1,), (1,)), ((), ())), preferred_element_type=jnp.float32
        ).astype(jnp.bfloat16)

    grad_normed = pair_firsts([feature], "llm")[0]
    scaled = grad_normed.reshape(tokens, own_count, VD) * gain
    projection = jnp.mean(scaled * local_x, axis=-1, keepdims=True)
    cubed = inverse * inverse * inverse
    grad_patches = (
        (inverse * scaled - local_x * cubed * projection)
        .reshape(tokens, own_count * VD)
        .astype(jnp.bfloat16)
    )
    return (image_embeds, grad_w_in, grad_w_out, grad_patches)


def solution(mesh):
    in_specs = (
        P("enc", "llm"),
        P(),
        P(None, "llm"),
        P("llm"),
        P("llm", None),
        P(),
        P(("enc", "llm"), None),
        P(("enc", "llm"), None),
    )
    out_specs = (P(("enc", "llm"), None), P("enc", "llm"), P("llm", "enc"), P("enc", "llm"))
    return jax.shard_map(local, mesh=mesh, in_specs=in_specs, out_specs=out_specs, check_vma=False)
```
